32 devices in a mesh: orig: 8 (over z, core), dest: 4 (over y, x).
Axes of the slice: x: 2, y: 2, z: 4, core: 2. Of those that a mesh axis runs over, the one named last changes fastest.
Arguments:
- counts: int32 [192, 48, 1024], P('orig', None, 'dest'), may hold values from 0 to 96, as said below
- anchor_factor: float32 [192, 32], P('orig'), may hold values from 0.3 to 3
- dest_factor: float32 [1024, 32], P(('dest', 'orig')), may hold values from 0.3 to 3
- hour_factor: float32 [48, 32], replicated, may hold values from 0.3 to 3
- weights: float32 [32], replicated, may hold values from 0.06 to 0.5
Outputs:
- anchor_out: float32 [192, 32], P('orig')
- dest_out: float32 [1024, 32], P(('dest', 'orig'))
- hour_out: float32 [48, 32], replicated
- weights_out: float32 [32], replicated
The draws below stay inside these ranges and needn't reach their ends.
Inputs may be any that keep to these rules, and one draw needn't show every extreme that they name: `counts`: whole numbers of trips; many entries are zero.
All inputs are finite; a program needn't handle non-finite values.
Results may differ from the reference program's by a relative error of at most 0.00015.
Values sent between devices are 32-bit elements; how exact they have to be, the bound alone decides.
A program may use at most 64 MiB of HBM per device.

```python
import math
import jax
import jax.numpy as jnp
from jax import lax

I_DEV = 24
K = 48
R = 32
INNER = 2
OUTER = 2
NI = 192
NJ = 1024
N_ORIG = 8


def draw_counts(key, part):
    subkeys = jax.random.split(jax.random.fold_in(key, 11), 4)
    anchor_exp = jax.random.randint(subkeys[0], (NI, 4), 0, 5, dtype=jnp.int32)
    hour_exp = jax.random.randint(subkeys[1], (K, 4), 0, 4, dtype=jnp.int32)
    dest_exp = jax.random.randint(subkeys[2], (NJ, 4), 0, 6, dtype=jnp.int32)
    anchor_level = jnp.left_shift(jnp.ones((NI, 4), jnp.int32), anchor_exp)
    hour_level = jnp.left_shift(jnp.ones((K, 4), jnp.int32), hour_exp)
    dest_level = jnp.left_shift(jnp.ones((NJ, 4), jnp.int32), dest_exp)
    total = jnp.zeros((NI, K, NJ), jnp.int32)
    for term in range(4):
        total = total + anchor_level[:, term][:, None, None] * hour_level[:, term][None, :, None] * dest_level[:, term][None, None, :]
    noise = jax.random.randint(subkeys[3], (NI, K, NJ), 0, 4, dtype=jnp.int32)
    return jnp.minimum(total * noise // 128, 96).astype(jnp.int32)


def block_scale(rng, dims, shards, least, high):
    factor_of, own = 1.0, jax.random.fold_in(rng, 6)
    for dim, shards_of in shards:
        draws = jnp.exp(jax.random.uniform(jax.random.fold_in(own, dim), (shards_of,), jnp.float32, least / len(shards), high / len(shards)))
        factor_of = factor_of * jnp.repeat(draws, dims[dim] // shards_of).reshape([-1 if axis == dim else 1 for axis in range(len(dims))])
    return factor_of


def setup_inputs(seed: int = 0) -> dict:
    key_list = jax.random.split(jax.random.key(seed), 6)
    return {
        "counts": draw_counts(jax.random.fold_in(key_list[5], 71), 0),
        "anchor_factor": jnp.clip(jnp.exp(math.log(3.0) - 2.3025851 * jax.random.uniform(key_list[1], (NI, R), jnp.float32) ** block_scale(key_list[1], (NI, R), ((0, 8),), -0.2, 0.2)), 0.3, 3.0),
        "dest_factor": jnp.clip(jnp.exp(math.log(3.0) - 2.3025851 * jax.random.uniform(key_list[2], (NJ, R), jnp.float32) ** block_scale(key_list[2], (NJ, R), ((0, 32),), -0.2, 0.2)), 0.3, 3.0),
        "hour_factor": jnp.clip(jnp.exp(jax.random.uniform(key_list[3], (K, R), jnp.float32, math.log(0.3), math.log(3.0))), 0.3, 3.0),
        "weights": jnp.clip(jnp.exp(jax.random.uniform(key_list[4], (R,), jnp.float32, math.log(0.06), math.log(0.5))), 0.06, 0.5),
    }


HIGH = lax.Precision.HIGHEST


def contract(counts, p_fac, q_fac, s_fac):
    blocks = counts.reshape(N_ORIG, I_DEV, K, NJ)
    p_blocks = p_fac.reshape(N_ORIG, I_DEV, R)

    def step(carry, item):
        block, p_part = item
        values = block.astype(jnp.float32).reshape(I_DEV * K, NJ)
        khatri = (p_part[:, None, :] * q_fac[None, :, :]).reshape(I_DEV * K, R)
        model = lax.dot_general(khatri, s_fac, (((1,), (1,)), ((), ())), precision=HIGH)
        ratio = values / model
        along = jnp.dot(ratio, s_fac, precision=HIGH).reshape(I_DEV, K, R)
        phi_i = jnp.sum(along * q_fac[None, :, :], axis=1)
        phi_k = jnp.sum(along * p_part[:, None, :], axis=0)
        phi_j = lax.dot_general(ratio, khatri, (((0,), (0,)), ((), ())), precision=HIGH)
        return (carry[0] + phi_k, carry[1] + phi_j), phi_i

    init = (jnp.zeros((K, R), jnp.float32), jnp.zeros((NJ, R), jnp.float32))
    (phi_k, phi_j), phi_i = lax.scan(step, init, (blocks, p_blocks))
    return phi_i.reshape(NI, R), phi_k, phi_j


def reference(counts, anchor_factor, dest_factor, hour_factor, weights):
    anchor, dest, hour, weight = anchor_factor, dest_factor, hour_factor, weights
    for outer in range(OUTER):
        growth = anchor * weight[None, :]
        for inner in range(INNER):
            phi_i, phi_k, phi_j = contract(counts, growth, hour, dest)
            growth = growth * (phi_i / (K * NJ))
        weight = jnp.sum(growth, axis=0) / NI
        anchor = growth / weight[None, :]
        growth = dest * weight[None, :]
        for inner in range(INNER):
            phi_i, phi_k, phi_j = contract(counts, anchor, hour, growth)
            growth = growth * (phi_j / (NI * K))
        weight = jnp.sum(growth, axis=0) / NJ
        dest = growth / weight[None, :]
        growth = hour * weight[None, :]
        for inner in range(INNER):
            phi_i, phi_k, phi_j = contract(counts, anchor, growth, dest)
            growth = growth * (phi_k / (NI * NJ))
        weight = jnp.sum(growth, axis=0) / K
        hour = growth / weight[None, :]
    return anchor, dest, hour, weight
```

```python
import functools

import jax
import jax.numpy as jnp
from jax import lax
from jax.experimental import pallas as pl
from jax.experimental.pallas import tpu as pltpu
from jax.sharding import PartitionSpec as P

INNER = 2
OUTER = 2
LANES = 128
F32 = jnp.float32
BF16 = jnp.bfloat16
HIGH = lax.Precision.HIGHEST
MESH = pl.DeviceIdType.MESH


def iota(shape, dim):
    return lax.broadcasted_iota(jnp.int32, shape, dim)


def kernel(nz, ndest, counts_ref, anchor_ref, dest_ref, hour_ref, weight_ref,
           anchor_out, dest_out, hour_out, weight_out,
           vals, outbox, ucur, ccur, tcur, bmod, balo, phis, acc, hacc,
           xbuf, zbuf, hbuf, abuf,
           x_send, x_recv, z_send, z_recv, h_send, h_recv, v_send, v_recv, a_sem):
    nrow, nhour, ncol = counts_ref.shape
    rank = hour_ref.shape[1]
    piece = dest_ref.shape[0]
    copies = LANES // rank
    half = ncol // 2
    nx = 2 * ndest
    total_rows = nrow * 2 * nz
    total_cols = ncol * ndest
    me_orig = lax.axis_index("orig")
    me_dest = lax.axis_index("dest")
    zi = me_orig // 2
    core = me_orig % 2
    xi = me_dest * 2 + core
    partner = {"orig": zi * 2 + (1 - core)}
    chunks = vals.shape[1] // (8 * nhour)
    crow = 8 * nhour

    def xpeer(t):
        idx = (xi + t) % nx
        return idx, {"orig": zi * 2 + idx % 2, "dest": idx // 2}

    def zpeer(t):
        idx = (zi + t) % nz
        return idx, {"orig": idx * 2 + core}

    barrier = pltpu.get_barrier_semaphore()
    for t in range(1, nx):
        pl.semaphore_signal(barrier, inc=1, device_id=xpeer(t)[1], device_id_type=MESH)
    for t in range(1, nz):
        pl.semaphore_signal(barrier, inc=1, device_id=zpeer(t)[1], device_id_type=MESH)

    def copy(ref, mine, theirs, send, recv, t, who):
        return pltpu.make_async_remote_copy(
            src_ref=ref.at[mine], dst_ref=ref.at[mine] if theirs is None else ref.at[theirs],
            send_sem=send.at[t - 1], recv_sem=recv.at[mine if theirs is None else theirs],
            device_id=who, device_id_type=MESH)

    def start(ref, send, recv, peer, n, me):
        for t in range(1, n):
            copy(ref, me, None, send, recv, t, peer(t)[1]).start()

    def collect(ref, send, recv, peer, n, me):
        for t in range(1, n):
            idx, who = peer(t)
            copy(ref, idx, None, send, recv, t, who).wait_recv()
        total = ref[0]
        for s in range(1, n):
            total = total + ref[s]
        return total

    def finish(ref, send, recv, peer, n, me):
        for t in range(1, n):
            copy(ref, me, None, send, recv, t, peer(t)[1]).wait_send()

    lane = iota((1, LANES), 1)
    group = lane // rank
    spread = (iota((rank, LANES), 1) % rank == iota((rank, LANES), 0)).astype(F32)
    diag = iota((rank, LANES), 1) == iota((rank, LANES), 0)
    diag_all = iota((rank, LANES), 1) % rank == iota((rank, LANES), 0)

    def to_column(row):
        return jnp.sum(jnp.where(diag, jnp.broadcast_to(row, (rank, LANES)), 0.0), axis=1, keepdims=True)

    def to_row(column):
        return jnp.sum(jnp.where(diag_all, jnp.broadcast_to(column, (rank, LANES)), 0.0), axis=0, keepdims=True)

    def spread_group(x, b):
        x = jnp.where(group == b, x, 0.0)
        step = rank
        while step < LANES:
            x = x + pltpu.roll(x, step, 1)
            step *= 2
        return x

    def pair_up(x):
        return x + pltpu.roll(x, rank, 1)

    def twice(x):
        return jnp.concatenate([x, x], axis=1)

    hrow = -(-nhour // (8 * (copies - 1))) * 8
    hblocks = nhour // hrow
    ablocks = nrow // 8

    def pack_hour(p, extra):
        out = jnp.broadcast_to(extra, (hrow, LANES))
        for b in range(hblocks):
            out = jnp.where(group == b, p[b * hrow:(b + 1) * hrow], out)
        return out

    def unpack_hour(s):
        return jnp.concatenate([spread_group(s, b) for b in range(hblocks)], axis=0)

    def pack_anchor(p):
        sides = []
        for g in range(2):
            side = p[:8, g * LANES:(g + 1) * LANES]
            for b in range(1, ablocks):
                side = jnp.where(group == b, p[8 * b:8 * b + 8, g * LANES:(g + 1) * LANES], side)
            sides.append(side)
        return jnp.concatenate(sides, axis=0)

    def unpack_anchor(s):
        sides = []
        for g in range(2):
            part = s[8 * g:8 * g + 8]
            sides.append(jnp.concatenate([spread_group(part, b) for b in range(ablocks)], axis=0))
        return jnp.concatenate(sides, axis=1)

    own_anchor = lax.dot(anchor_ref[...], spread, precision=HIGH)
    weight_row = jnp.sum(jnp.where(
        diag_all, jnp.broadcast_to(to_rows(weight_ref[...], rank), (rank, LANES)), 0.0), axis=0, keepdims=True)
    abuf[core] = own_anchor * weight_row
    ccur[...] = twice(lax.dot(hour_ref[...], spread, precision=HIGH))
    place = (iota((piece, LANES), 1) == zi * piece + iota((piece, LANES), 0)).astype(F32)
    zbuf[0, zi] = jnp.concatenate([
        lax.dot_general(dest_ref[...], place, (((0,), (0,)), ((), ())), precision=HIGH),
        jnp.zeros((8, LANES), F32)], axis=0)

    dst = iota((ncol, ncol), 1)
    src = iota((ncol, ncol), 0)
    local = dst % half
    side = dst // half
    parity = (core + side) % 2
    wanted = local + (local // piece + parity) * piece
    perm = (src == wanted).astype(F32).astype(BF16)

    pl.semaphore_wait(barrier, nx - 1 + nz - 1)

    start(zbuf.at[0], z_send.at[0], z_recv.at[0], zpeer, nz, zi)

    def acopy(slot):
        return pltpu.make_async_remote_copy(
            src_ref=abuf.at[slot], dst_ref=abuf.at[slot], send_sem=a_sem.at[0], recv_sem=a_sem.at[1],
            device_id=partner, device_id_type=MESH)

    acopy(core).start()

    def vcopy(s, slot):
        return pltpu.make_async_remote_copy(
            src_ref=outbox.at[pl.ds(s * crow, crow)],
            dst_ref=vals.at[slot, pl.ds(s * crow, crow)],
            send_sem=v_send.at[s], recv_sem=v_recv.at[s],
            device_id=partner, device_id_type=MESH)

    for s in range(chunks):
        block = counts_ref[8 * s:8 * s + 8].reshape(crow, ncol).astype(F32).astype(BF16)
        moved = jnp.dot(block, perm, preferred_element_type=F32)
        outbox[s * crow:(s + 1) * crow] = moved[:, half:]
        vals[core, s * crow:(s + 1) * crow] = moved[:, :half]
        vcopy(s, core).start()

    zero = jnp.zeros((LANES, LANES), BF16)
    for ref in (bmod, balo):
        ref[:LANES, LANES:] = zero
        ref[LANES:, :LANES] = zero

    def set_right(t):
        hi = t.astype(BF16).astype(F32)
        lo = t - hi
        model = jnp.concatenate([hi] * (copies // 2) + [lo] * (copies // 2), axis=0).astype(BF16)
        along = jnp.concatenate([hi, lo] * (copies // 2), axis=0).astype(BF16)
        for ref, x in ((bmod, model), (balo, along)):
            ref[:LANES, :LANES] = x
            ref[LANES:, LANES:] = x

    high_lane = (iota((1, 2 * LANES), 1) // rank) % 2 == 0

    def ratio_chunk(s):
        i0 = pl.multiple_of(s * 8, 8)
        r0 = pl.multiple_of(s * crow, crow)
        left = ucur[pl.ds(i0, 8), :]
        kh = (left[:, None, :] * ccur[...][None, :, :]).reshape(crow, 2 * LANES)
        hi = kh.astype(BF16).astype(F32)
        khs = jnp.where(high_lane, hi, kh - hi).astype(BF16)
        model = jnp.dot(khs, bmod[...], preferred_element_type=F32)
        values = jnp.concatenate([vals[0, pl.ds(r0, crow), :], vals[1, pl.ds(r0, crow), :]], axis=1)
        ratio = values / model
        rh = ratio.astype(BF16)
        rl = (ratio - rh.astype(F32)).astype(BF16)
        return i0, left, khs, rh, rl

    def along_of(rh, rl):
        dims = (((1,), (1,)), ((), ()))
        return (lax.dot_general(rh, balo[...], dims, preferred_element_type=F32)
                + lax.dot_general(rl, balo[...], dims, preferred_element_type=F32))

    def anchor_phi():
        @pl.loop(0, chunks)
        def _(s):
            i0, left, khs, rh, rl = ratio_chunk(s)
            along = along_of(rh, rl).reshape(8, nhour, 2 * LANES)
            phis[pl.ds(i0, 8), :] = jnp.sum(along * ccur[...][None, :, :], axis=1)
        p = phis[...]
        return jnp.concatenate([pair_up(p[:, :LANES]), pair_up(p[:, LANES:])], axis=1)

    def hour_phi():
        hacc[...] = jnp.zeros_like(hacc)

        @pl.loop(0, chunks)
        def _(s):
            i0, left, khs, rh, rl = ratio_chunk(s)
            along = along_of(rh, rl).reshape(8, nhour, 2 * LANES)
            hacc[...] += jnp.sum(along * left[:, None, :], axis=0)
        p = hacc[...]
        return pair_up(p[:, :LANES] + p[:, LANES:])

    def dest_phi():
        acc[...] = jnp.zeros_like(acc)
        dims = (((0,), (0,)), ((), ()))

        @pl.loop(0, chunks)
        def _(s):
            i0, left, khs, rh, rl = ratio_chunk(s)
            total = acc[...]
            for g in range(2):
                lanes = slice(g * LANES, (g + 1) * LANES)
                total = total + lax.dot_general(khs[:, lanes], rh[:, lanes], dims, preferred_element_type=F32)
                total = total + lax.dot_general(khs[:, lanes], rl[:, lanes], dims, preferred_element_type=F32)
            acc[...] = total
        return acc[:rank] + acc[rank:2 * rank]

    acopy(1 - core).wait_recv()
    ucur[...] = jnp.concatenate([abuf[0], abuf[1]], axis=1)
    gathered = collect(zbuf.at[0], z_send.at[0], z_recv.at[0], zpeer, nz, zi)
    tcur[...] = gathered[:rank]
    set_right(tcur[...])
    for s in range(chunks):
        vcopy(s, 1 - core).wait_recv()

    @pl.loop(0, OUTER)
    def _(outer):
        for inner in range(INNER):
            e = outer * 4 + inner
            xb, xs, xr = xbuf.at[e], x_send.at[e], x_recv.at[e]
            xb[xi] = pack_anchor(anchor_phi())
            start(xb, xs, xr, xpeer, nx, xi)
            s = collect(xb, xs, xr, xpeer, nx, xi)
            ucur[...] = ucur[...] * (unpack_anchor(s) / (nhour * total_cols))
        col = jnp.sum(ucur[...], axis=0, keepdims=True)
        col = col[:, :LANES] + col[:, LANES:]
        anchor_w = None
        for inner in range(INNER):
            e = 1 + outer * 2 + inner
            zb, zs, zr = zbuf.at[e], z_send.at[e], z_recv.at[e]
            zb[zi] = jnp.concatenate([dest_phi(), jnp.broadcast_to(col, (8, LANES))], axis=0)
            start(zb, zs, zr, zpeer, nz, zi)
            s = collect(zb, zs, zr, zpeer, nz, zi)
            growth = tcur[...] * (s[:rank] / (total_rows * nhour))
            if inner == 0:
                anchor_w = s[rank:rank + 1] / total_rows
                growth = growth / to_column(anchor_w)
            tcur[...] = growth
            set_right(growth)
        ucur[...] = ucur[...] / twice(anchor_w)
        dest_col = to_row(jnp.sum(tcur[...], axis=1, keepdims=True))
        dest_w = None
        for inner in range(INNER):
            e = outer * 4 + 2 + inner
            xb, xs, xr = xbuf.at[e], x_send.at[e], x_recv.at[e]
            xb[xi] = pack_hour(hour_phi(), dest_col)
            start(xb, xs, xr, xpeer, nx, xi)
            s = collect(xb, xs, xr, xpeer, nx, xi)
            h = outer * 2 + inner
            hb, hs, hr = hbuf.at[h], h_send.at[h], h_recv.at[h]
            hb[zi] = s
            start(hb, hs, hr, zpeer, nz, zi)
            if inner == 0:
                dest_w = spread_group(s[:1], copies - 1) / total_cols
            s = collect(hb, hs, hr, zpeer, nz, zi)
            growth = ccur[:, :LANES] * (unpack_hour(s) / (total_rows * total_cols))
            if inner == 0:
                growth = growth / dest_w
            ccur[...] = twice(growth)
        w = jnp.sum(ccur[:, :LANES], axis=0, keepdims=True) / nhour
        ccur[...] = ccur[...] / twice(w)
        tcur[...] = tcur[...] / to_column(dest_w)
        weight_out[...] = w[:, :rank]

        @pl.when(outer == OUTER - 1)
        def _():
            mine = jnp.where(core == 0, ucur[:, :LANES], ucur[:, LANES:])
            anchor_out[...] = mine[:, :rank]
            hour_out[...] = ccur[:, :rank]
            dest_out[...] = lax.dot_general(
                place, tcur[...], (((1,), (1,)), ((), ())), precision=HIGH)

        @pl.when(outer < OUTER - 1)
        def _():
            ucur[...] = ucur[...] * twice(w)
            set_right(tcur[...])

    acopy(core).wait_send()
    for s in range(chunks):
        vcopy(s, core).wait_send()
    finish(zbuf.at[0], z_send.at[0], z_recv.at[0], zpeer, nz, zi)

    @pl.loop(0, OUTER * 4)
    def _(e):
        finish(xbuf.at[e], x_send.at[e], x_recv.at[e], xpeer, nx, xi)

    @pl.loop(0, OUTER * 2)
    def _(e):
        finish(zbuf.at[1 + e], z_send.at[1 + e], z_recv.at[1 + e], zpeer, nz, zi)
        finish(hbuf.at[e], h_send.at[e], h_recv.at[e], zpeer, nz, zi)


def to_rows(row, rank):
    square = jnp.where(iota((rank, rank), 0) == iota((rank, rank), 1), jnp.broadcast_to(row, (rank, rank)), 0.0)
    return jnp.sum(square, axis=1, keepdims=True)


def on_device(counts, anchor_factor, dest_factor, hour_factor, weights):
    norig = lax.axis_size("orig")
    ndest = lax.axis_size("dest")
    nz, nx = norig // 2, 2 * ndest
    nrow, nhour, ncol = counts.shape
    rank = hour_factor.shape[1]
    rows = nrow * nhour
    chunks = nrow // 8
    hrow = -(-nhour // (8 * (LANES // rank - 1))) * 8
    dma = pltpu.SemaphoreType.DMA
    vmem = pltpu.VMEM
    outs = pl.pallas_call(
        functools.partial(kernel, nz, ndest),
        out_shape=[
            jax.ShapeDtypeStruct(anchor_factor.shape, F32),
            jax.ShapeDtypeStruct(dest_factor.shape, F32),
            jax.ShapeDtypeStruct(hour_factor.shape, F32),
            jax.ShapeDtypeStruct((1, rank), F32),
        ],
        in_specs=[pl.BlockSpec(memory_space=pltpu.VMEM)] * 5,
        out_specs=[pl.BlockSpec(memory_space=pltpu.VMEM)] * 4,
        scratch_shapes=[
            vmem((2, rows, LANES), F32),
            vmem((rows, LANES), F32),
            vmem((nrow, 2 * LANES), F32),
            vmem((nhour, 2 * LANES), F32),
            vmem((rank, LANES), F32),
            vmem((2 * LANES, 2 * LANES), BF16),
            vmem((2 * LANES, 2 * LANES), BF16),
            vmem((nrow, 2 * LANES), F32),
            vmem((LANES, LANES), F32),
            vmem((nhour, 2 * LANES), F32),
            vmem((OUTER * 4, nx, hrow, LANES), F32),
            vmem((1 + OUTER * 2, nz, rank + 8, LANES), F32),
            vmem((OUTER * 2, nz, hrow, LANES), F32),
            vmem((2, nrow, LANES), F32),
            dma((OUTER * 4, nx - 1)), dma((OUTER * 4, nx)),
            dma((1 + OUTER * 2, nz - 1)), dma((1 + OUTER * 2, nz)),
            dma((OUTER * 2, nz - 1)), dma((OUTER * 2, nz)),
            dma((chunks,)), dma((chunks,)), dma((2,)),
        ],
        compiler_params=pltpu.CompilerParams(
            collective_id=0, has_side_effects=True, vmem_limit_bytes=48 * 1024 * 1024),
    )(counts, anchor_factor, dest_factor, hour_factor, weights.reshape(1, rank))
    return outs[0], outs[1], outs[2], outs[3].reshape(rank)


def solution(mesh):
    return jax.shard_map(
        on_device,
        mesh=mesh,
        in_specs=(P("orig", None, "dest"), P("orig", None), P(("dest", "orig"), None), P(), P()),
        out_specs=(P("orig", None), P(("dest", "orig"), None), P(), P()),
        check_vma=False,
    )
```

```python
import functools

import jax
import jax.numpy as jnp
from jax import lax
from jax.experimental import pallas as pl
from jax.experimental.pallas import tpu as pltpu
from jax.sharding import PartitionSpec as P

INNER = 2
OUTER = 2
LANES = 128
F32 = jnp.float32
BF16 = jnp.bfloat16
HIGH = lax.Precision.HIGHEST
MESH = pl.DeviceIdType.MESH


def iota(shape, dim):
    return lax.broadcasted_iota(jnp.int32, shape, dim)


def kernel(nz, ndest, counts_in, anchor_in, dest_in, hour_in, weight_in,
           anchor_out, dest_out, hour_out, weight_out,
           vals, outbox, ucur, ccur, tcur, bmod, balo,
           xbuf, zbuf, hbuf, abuf, counts_ref, anchor_ref, dest_ref, hour_ref, weight_ref,
           x_send, x_recv, z_send, z_recv, h_send, h_recv, v_send, v_recv, a_sem, in_sem):
    nrow, nhour, ncol = counts_ref.shape
    rank = hour_ref.shape[0]
    piece = dest_ref.shape[0]
    copies = LANES // rank
    half = ncol // 2
    nx = 2 * ndest
    total_rows = nrow * 2 * nz
    total_cols = ncol * ndest
    me_orig = lax.axis_index("orig")
    me_dest = lax.axis_index("dest")
    zi = me_orig // 2
    core = me_orig % 2
    xi = me_dest * 2 + core
    partner = {"orig": zi * 2 + (1 - core)}
    chunks = vals.shape[1] // (8 * nhour)
    crow = 8 * nhour

    def xpeer(t):
        idx = (xi + t) % nx
        return idx, {"orig": zi * 2 + idx % 2, "dest": idx // 2}

    def zpeer(t):
        idx = (zi + t) % nz
        return idx, {"orig": idx * 2 + core}

    small = [pltpu.make_async_copy(a, b, in_sem.at[q]) for q, (a, b) in enumerate(
        ((anchor_in, anchor_ref), (dest_in, dest_ref), (hour_in, hour_ref), (weight_in, weight_ref)))]
    large = [pltpu.make_async_copy(counts_in.at[pl.ds(8 * s, 8)], counts_ref.at[pl.ds(8 * s, 8)], in_sem.at[4 + s])
             for s in range(chunks)]
    for dma in small + large:
        dma.start()
    barrier = pltpu.get_barrier_semaphore()
    for t in range(1, nx):
        pl.semaphore_signal(barrier, inc=1, device_id=xpeer(t)[1], device_id_type=MESH)
    for t in range(1, nz):
        pl.semaphore_signal(barrier, inc=1, device_id=zpeer(t)[1], device_id_type=MESH)

    def copy(ref, mine, theirs, send, recv, t, who):
        return pltpu.make_async_remote_copy(
            src_ref=ref.at[mine], dst_ref=ref.at[mine] if theirs is None else ref.at[theirs],
            send_sem=send.at[t - 1], recv_sem=recv.at[mine if theirs is None else theirs],
            device_id=who, device_id_type=MESH)

    def start(ref, send, recv, peer, n, me):
        for t in range(1, n):
            copy(ref, me, None, send, recv, t, peer(t)[1]).start()

    def collect(ref, send, recv, peer, n, me):
        for t in range(1, n):
            idx, who = peer(t)
            copy(ref, idx, None, send, recv, t, who).wait_recv()
        total = ref[0]
        for s in range(1, n):
            total = total + ref[s]
        return total

    def finish(ref, send, recv, peer, n, me):
        for t in range(1, n):
            copy(ref, me, None, send, recv, t, peer(t)[1]).wait_send()

    lane = iota((1, LANES), 1)
    group = lane // rank
    spread = (iota((rank, LANES), 1) % rank == iota((rank, LANES), 0)).astype(F32)
    diag = iota((rank, LANES), 1) == iota((rank, LANES), 0)
    diag_all = iota((rank, LANES), 1) % rank == iota((rank, LANES), 0)

    def to_column(row):
        return jnp.sum(jnp.where(diag, jnp.broadcast_to(row, (rank, LANES)), 0.0), axis=1, keepdims=True)

    def to_row(column):
        return jnp.sum(jnp.where(diag_all, jnp.broadcast_to(column, (rank, LANES)), 0.0), axis=0, keepdims=True)

    def spread_group(x, b):
        x = jnp.where(group == b, x, 0.0)
        step = rank
        while step < LANES:
            x = x + pltpu.roll(x, step, 1)
            step *= 2
        return x

    def pair_up(x):
        return x + pltpu.roll(x, rank, 1)

    def twice(x):
        return jnp.concatenate([x, x], axis=1)

    hrow = -(-nhour // (8 * (copies - 1))) * 8
    hblocks = nhour // hrow
    ablocks = nrow // 8

    def pack_hour(p, extra):
        out = jnp.broadcast_to(extra, (hrow, LANES))
        for b in range(hblocks):
            out = jnp.where(group == b, p[b * hrow:(b + 1) * hrow], out)
        return out

    def unpack_hour(s):
        return jnp.concatenate([spread_group(s, b) for b in range(hblocks)], axis=0)

    def pack_anchor(p):
        sides = []
        for g in range(2):
            side = p[:8, g * LANES:(g + 1) * LANES]
            for b in range(1, ablocks):
                side = jnp.where(group == b, p[8 * b:8 * b + 8, g * LANES:(g + 1) * LANES], side)
            sides.append(side)
        return jnp.concatenate(sides, axis=0)

    def unpack_anchor(s):
        sides = []
        for g in range(2):
            part = s[8 * g:8 * g + 8]
            sides.append(jnp.concatenate([spread_group(part, b) for b in range(ablocks)], axis=0))
        return jnp.concatenate(sides, axis=1)

    dst = iota((ncol, ncol), 1)
    src = iota((ncol, ncol), 0)
    local = dst % half
    side = dst // half
    parity = (core + side) % 2
    wanted = local + (local // piece + parity) * piece
    perm = (src == wanted).astype(F32).astype(BF16)

    def arrange(s):
        large[s].wait()
        block = counts_ref[8 * s:8 * s + 8].reshape(crow, ncol).astype(F32).astype(BF16)
        moved = jnp.dot(block, perm, preferred_element_type=F32)
        outbox[s * crow:(s + 1) * crow] = moved[:, half:]
        vals[core, s * crow:(s + 1) * crow] = moved[:, :half]

    for dma in small:
        dma.wait()
    own_anchor = lax.dot(anchor_ref[...], spread, precision=HIGH)
    weight_row = jnp.sum(jnp.where(
        diag_all, jnp.broadcast_to(to_rows(weight_ref[...], rank), (rank, LANES)), 0.0), axis=0, keepdims=True)
    abuf[core] = own_anchor * weight_row
    ccur[...] = twice(lax.dot_general(hour_ref[...], spread, (((0,), (0,)), ((), ())), precision=HIGH))
    place = (iota((piece, LANES), 1) == zi * piece + iota((piece, LANES), 0)).astype(F32)
    zbuf[0, zi] = jnp.concatenate([
        lax.dot_general(dest_ref[...], place, (((0,), (0,)), ((), ())), precision=HIGH),
        jnp.zeros((8, LANES), F32)], axis=0)

    pl.semaphore_wait(barrier, nx - 1 + nz - 1)

    start(zbuf.at[0], z_send.at[0], z_recv.at[0], zpeer, nz, zi)

    def acopy(slot):
        return pltpu.make_async_remote_copy(
            src_ref=abuf.at[slot], dst_ref=abuf.at[slot], send_sem=a_sem.at[0], recv_sem=a_sem.at[1],
            device_id=partner, device_id_type=MESH)

    acopy(core).start()

    def vcopy(s, slot):
        return pltpu.make_async_remote_copy(
            src_ref=outbox.at[pl.ds(s * crow, crow)],
            dst_ref=vals.at[slot, pl.ds(s * crow, crow)],
            send_sem=v_send.at[s], recv_sem=v_recv.at[s],
            device_id=partner, device_id_type=MESH)

    for s in range(chunks):
        arrange(s)
        vcopy(s, core).start()

    bmod[...] = jnp.zeros_like(bmod)
    balo[...] = jnp.zeros_like(balo)

    def set_right(t):
        hi = t.astype(BF16).astype(F32)
        lo = t - hi
        model = jnp.concatenate([hi] * (copies // 2) + [lo] * (copies // 2), axis=0).astype(BF16)
        along = jnp.concatenate([hi, lo], axis=0).astype(BF16)
        for g in range(2):
            lanes = slice(g * LANES, (g + 1) * LANES)
            bmod[lanes, lanes] = model
            for part in range(2):
                balo[g * 2 * rank:(g + 1) * 2 * rank, (2 * part + g) * LANES:(2 * part + g + 1) * LANES] = along

    high_lane = (iota((1, 2 * LANES), 1) // rank) % 2 == 0

    def ratio_chunk(s):
        left = ucur[8 * s:8 * s + 8]
        kh = (left[:, None, :] * ccur[...][None, :, :]).reshape(crow, 2 * LANES)
        hi = kh.astype(BF16).astype(F32)
        khs = jnp.where(high_lane, hi, kh - hi).astype(BF16)
        model = jnp.dot(khs, bmod[...], preferred_element_type=F32)
        rows = slice(s * crow, (s + 1) * crow)
        values = jnp.concatenate([vals[0, rows], vals[1, rows]], axis=1)
        ratio = values / model
        rh = ratio.astype(BF16)
        rl = (ratio - rh.astype(F32)).astype(BF16)
        return left, khs, rh, rl

    def along_of(rh, rl):
        return lax.dot_general(jnp.concatenate([rh, rl], axis=1), balo[...], (((1,), (1,)), ((), ())),
                               preferred_element_type=F32).reshape(8, nhour, LANES)

    def anchor_phi():
        parts = []
        for s in range(chunks):
            left, khs, rh, rl = ratio_chunk(s)
            parts.append(jnp.sum(along_of(rh, rl) * ccur[:, :LANES][None, :, :], axis=1))
        p = pair_up(jnp.concatenate(parts, axis=0))
        return jnp.concatenate([spread_group(p, 1), spread_group(p, 3)], axis=1)

    def hour_phi():
        p = None
        for s in range(chunks):
            left, khs, rh, rl = ratio_chunk(s)
            mixed = jnp.where(group < 2, left[:, :LANES], left[:, LANES:])
            part = jnp.sum(along_of(rh, rl) * mixed[:, None, :], axis=0)
            p = part if p is None else p + part
        return pair_up(p + pltpu.roll(p, 2 * rank, 1))

    def dest_phi():
        dims = (((0,), (0,)), ((), ()))
        total = None
        for s in range(chunks):
            left, khs, rh, rl = ratio_chunk(s)
            for g in range(2):
                lanes = slice(g * LANES, (g + 1) * LANES)
                for r in (rh, rl):
                    part = lax.dot_general(khs[:, lanes], r[:, lanes], dims, preferred_element_type=F32)
                    total = part if total is None else total + part
        return total[:rank] + total[rank:2 * rank]

    acopy(1 - core).wait_recv()
    ucur[...] = jnp.concatenate([abuf[0], abuf[1]], axis=1)
    gathered = collect(zbuf.at[0], z_send.at[0], z_recv.at[0], zpeer, nz, zi)
    tcur[...] = gathered[:rank]
    set_right(tcur[...])
    for s in range(chunks):
        vcopy(s, 1 - core).wait_recv()

    @pl.loop(0, OUTER)
    def _(outer):
        for inner in range(INNER):
            e = outer * 4 + inner
            xb, xs, xr = xbuf.at[e], x_send.at[e], x_recv.at[e]
            xb[xi] = pack_anchor(anchor_phi())
            start(xb, xs, xr, xpeer, nx, xi)
            s = collect(xb, xs, xr, xpeer, nx, xi)
            ucur[...] = ucur[...] * (unpack_anchor(s) / (nhour * total_cols))
        col = jnp.sum(ucur[...], axis=0, keepdims=True)
        col = col[:, :LANES] + col[:, LANES:]
        anchor_w = None
        for inner in range(INNER):
            e = 1 + outer * 2 + inner
            zb, zs, zr = zbuf.at[e], z_send.at[e], z_recv.at[e]
            zb[zi] = jnp.concatenate([dest_phi(), jnp.broadcast_to(col, (8, LANES))], axis=0)
            start(zb, zs, zr, zpeer, nz, zi)
            s = collect(zb, zs, zr, zpeer, nz, zi)
            growth = tcur[...] * (s[:rank] / (total_rows * nhour))
            if inner == 0:
                anchor_w = s[rank:rank + 1] / total_rows
                growth = growth / to_column(anchor_w)
            tcur[...] = growth
            set_right(growth)
        ucur[...] = ucur[...] / twice(anchor_w)
        dest_col = to_row(jnp.sum(tcur[...], axis=1, keepdims=True))
        dest_w = None
        for inner in range(INNER):
            e = outer * 4 + 2 + inner
            xb, xs, xr = xbuf.at[e], x_send.at[e], x_recv.at[e]
            xb[xi] = pack_hour(hour_phi(), dest_col)
            start(xb, xs, xr, xpeer, nx, xi)
            s = collect(xb, xs, xr, xpeer, nx, xi)
            h = outer * 2 + inner
            hb, hs, hr = hbuf.at[h], h_send.at[h], h_recv.at[h]
            hb[zi] = s
            start(hb, hs, hr, zpeer, nz, zi)
            if inner == 0:
                dest_w = spread_group(s[:1], copies - 1) / total_cols
            s = collect(hb, hs, hr, zpeer, nz, zi)
            growth = ccur[:, :LANES] * (unpack_hour(s) / (total_rows * total_cols))
            if inner == 0:
                growth = growth / dest_w
            ccur[...] = twice(growth)
        w = jnp.sum(ccur[:, :LANES], axis=0, keepdims=True) / nhour
        ccur[...] = ccur[...] / twice(w)
        tcur[...] = tcur[...] / to_column(dest_w)
        weight_out[...] = w[:, :rank]

        @pl.when(outer == OUTER - 1)
        def _():
            mine = jnp.where(core == 0, ucur[:, :LANES], ucur[:, LANES:])
            anchor_out[...] = mine[:, :rank]
            hour_out[...] = lax.dot_general(
                diag.astype(F32), ccur[:, :LANES], (((1,), (1,)), ((), ())), precision=HIGH)
            dest_out[...] = lax.dot_general(
                place, tcur[...], (((1,), (1,)), ((), ())), precision=HIGH)

        @pl.when(outer < OUTER - 1)
        def _():
            ucur[...] = ucur[...] * twice(w)
            set_right(tcur[...])

    acopy(core).wait_send()
    for s in range(chunks):
        vcopy(s, core).wait_send()
    finish(zbuf.at[0], z_send.at[0], z_recv.at[0], zpeer, nz, zi)

    @pl.loop(0, OUTER * 4)
    def _(e):
        finish(xbuf.at[e], x_send.at[e], x_recv.at[e], xpeer, nx, xi)

    @pl.loop(0, OUTER * 2)
    def _(e):
        finish(zbuf.at[1 + e], z_send.at[1 + e], z_recv.at[1 + e], zpeer, nz, zi)
        finish(hbuf.at[e], h_send.at[e], h_recv.at[e], zpeer, nz, zi)


def put_out(*refs):
    copies = [pltpu.make_async_copy(refs[q], refs[4 + q], refs[8].at[q]) for q in range(4)]
    for c in copies:
        c.start()
    for c in copies:
        c.wait()


def to_rows(row, rank):
    square = jnp.where(iota((rank, rank), 0) == iota((rank, rank), 1), jnp.broadcast_to(row, (rank, rank)), 0.0)
    return jnp.sum(square, axis=1, keepdims=True)


def on_device(counts, anchor_factor, dest_factor, hour_factor, weights):
    norig = lax.axis_size("orig")
    ndest = lax.axis_size("dest")
    nz, nx = norig // 2, 2 * ndest
    nrow, nhour, ncol = counts.shape
    rank = hour_factor.shape[1]
    rows = nrow * nhour
    chunks = nrow // 8
    hrow = -(-nhour // (8 * (LANES // rank - 1))) * 8
    dma = pltpu.SemaphoreType.DMA
    vmem = pltpu.VMEM
    outs = pl.pallas_call(
        functools.partial(kernel, nz, ndest),
        out_shape=[
            jax.ShapeDtypeStruct(anchor_factor.shape, F32),
            jax.ShapeDtypeStruct(dest_factor.shape, F32),
            jax.ShapeDtypeStruct((rank, nhour), F32),
            jax.ShapeDtypeStruct((1, rank), F32),
        ],
        in_specs=[pl.BlockSpec(memory_space=pltpu.HBM)] * 5,
        out_specs=[pl.BlockSpec(memory_space=pltpu.VMEM)] * 4,
        scratch_shapes=[
            vmem((2, rows, LANES), F32),
            vmem((rows, LANES), F32),
            vmem((nrow, 2 * LANES), F32),
            vmem((nhour, 2 * LANES), F32),
            vmem((rank, LANES), F32),
            vmem((2 * LANES, 2 * LANES), BF16),
            vmem((4 * rank, 4 * LANES), BF16),
            vmem((OUTER * 4, nx, hrow, LANES), F32),
            vmem((1 + OUTER * 2, nz, rank + 8, LANES), F32),
            vmem((OUTER * 2, nz, hrow, LANES), F32),
            vmem((2, nrow, LANES), F32),
            vmem(counts.shape, counts.dtype),
            vmem(anchor_factor.shape, F32),
            vmem(dest_factor.shape, F32),
            vmem((rank, nhour), F32),
            vmem((1, rank), F32),
            dma((OUTER * 4, nx - 1)), dma((OUTER * 4, nx)),
            dma((1 + OUTER * 2, nz - 1)), dma((1 + OUTER * 2, nz)),
            dma((OUTER * 2, nz - 1)), dma((OUTER * 2, nz)),
            dma((chunks,)), dma((chunks,)), dma((2,)), dma((4 + chunks,)),
        ],
        compiler_params=pltpu.CompilerParams(
            collective_id=0, has_side_effects=True, vmem_limit_bytes=67043328),
    )(counts, anchor_factor, dest_factor, hour_factor.T, weights.reshape(1, rank))
    outs = pl.pallas_call(
        put_out,
        out_shape=[jax.ShapeDtypeStruct(o.shape, F32) for o in outs],
        in_specs=[pl.BlockSpec(memory_space=pltpu.VMEM)] * 4,
        out_specs=[pl.BlockSpec(memory_space=pltpu.HBM)] * 4,
        scratch_shapes=[dma((4,))],
    )(*outs)
    return outs[0], outs[1], outs[2].T, outs[3].reshape(rank)


def solution(mesh):
    return jax.shard_map(
        on_device,
        mesh=mesh,
        in_specs=(P("orig", None, "dest"), P("orig", None), P(("dest", "orig"), None), P(), P()),
        out_specs=(P("orig", None), P(("dest", "orig"), None), P(), P()),
        check_vma=False,
    )
```

```python
import functools

import jax
import jax.numpy as jnp
from jax import lax
from jax.experimental import pallas as pl
from jax.experimental.pallas import tpu as pltpu
from jax.sharding import PartitionSpec as P

INNER = 2
OUTER = 2
LANES = 128
F32 = jnp.float32
BF16 = jnp.bfloat16
HIGH = lax.Precision.HIGHEST
MESH = pl.DeviceIdType.MESH


def iota(shape, dim):
    return lax.broadcasted_iota(jnp.int32, shape, dim)


def kernel(nz, ndest, counts_in, anchor_in, dest_in, hour_in, weight_in,
           anchor_out, dest_out, hour_out, weight_out,
           vals, outbox, ucur, ccur, tcur, bmod, balo,
           xbuf, zbuf, hbuf, abuf, counts_ref, anchor_ref, dest_ref, hour_ref, weight_ref,
           x_send, x_recv, z_send, z_recv, h_send, h_recv, v_send, v_recv, a_sem, in_sem):
    nrow, nhour, ncol = counts_ref.shape
    rank = hour_ref.shape[0]
    piece = dest_ref.shape[0]
    copies = LANES // rank
    half = ncol // 2
    nx = 2 * ndest
    total_rows = nrow * 2 * nz
    total_cols = ncol * ndest
    me_orig = lax.axis_index("orig")
    me_dest = lax.axis_index("dest")
    zi = me_orig // 2
    core = me_orig % 2
    xi = me_dest * 2 + core
    partner = {"orig": zi * 2 + (1 - core)}
    chunks = vals.shape[1] // (8 * nhour)
    crow = 8 * nhour

    xpeers = []
    for t in range(1, nx):
        idx = (xi + t) % nx
        xpeers.append({"orig": zi * 2 + idx % 2, "dest": idx // 2})
    zpeers = [{"orig": (zi + t) % nz * 2 + core} for t in range(1, nz)]

    small = [pltpu.make_async_copy(a, b, in_sem.at[q]) for q, (a, b) in enumerate(
        ((anchor_in, anchor_ref), (dest_in, dest_ref), (hour_in, hour_ref), (weight_in, weight_ref)))]
    large = [pltpu.make_async_copy(counts_in.at[pl.ds(8 * s, 8)], counts_ref.at[pl.ds(8 * s, 8)], in_sem.at[4 + s])
             for s in range(chunks)]
    for dma in small + large:
        dma.start()
    barrier = pltpu.get_barrier_semaphore()
    for who in zpeers + xpeers:
        pl.semaphore_signal(barrier, inc=1, device_id=who, device_id_type=MESH)

    def start(ref, send, recv, peers, me):
        for who in peers:
            pltpu.make_async_remote_copy(
                src_ref=ref.at[me], dst_ref=ref.at[me], send_sem=send, recv_sem=recv,
                device_id=who, device_id_type=MESH).start()

    def wait_bytes(ref, sem):
        pltpu.make_async_copy(ref, ref, sem).wait()

    def collect(ref, recv, n):
        wait_bytes(ref.at[pl.ds(0, n - 1)], recv)
        total = ref[0]
        for s in range(1, n):
            total = total + ref[s]
        return total

    lane = iota((1, LANES), 1)
    group = lane // rank
    spread = (iota((rank, LANES), 1) % rank == iota((rank, LANES), 0)).astype(F32)
    diag = iota((rank, LANES), 1) == iota((rank, LANES), 0)
    diag_all = iota((rank, LANES), 1) % rank == iota((rank, LANES), 0)

    def to_column(row):
        return jnp.sum(jnp.where(diag, jnp.broadcast_to(row, (rank, LANES)), 0.0), axis=1, keepdims=True)

    def to_row(column):
        return jnp.sum(jnp.where(diag_all, jnp.broadcast_to(column, (rank, LANES)), 0.0), axis=0, keepdims=True)

    def spread_group(x, b):
        x = jnp.where(group == b, x, 0.0)
        step = rank
        while step < LANES:
            x = x + pltpu.roll(x, step, 1)
            step *= 2
        return x

    def pair_up(x):
        return x + pltpu.roll(x, rank, 1)

    def twice(x):
        return jnp.concatenate([x, x], axis=1)

    hrow = -(-nhour // (8 * (copies - 1))) * 8
    hblocks = nhour // hrow
    ablocks = nrow // 8

    def pack_hour(p, extra):
        out = jnp.broadcast_to(extra, (hrow, LANES))
        for b in range(hblocks):
            out = jnp.where(group == b, p[b * hrow:(b + 1) * hrow], out)
        return out

    def unpack_hour(s):
        return jnp.concatenate([spread_group(s, b) for b in range(hblocks)], axis=0)

    def pack_anchor(p):
        sides = []
        for g in range(2):
            side = p[:8, g * LANES:(g + 1) * LANES]
            for b in range(1, ablocks):
                side = jnp.where(group == b, p[8 * b:8 * b + 8, g * LANES:(g + 1) * LANES], side)
            sides.append(side)
        return jnp.concatenate(sides, axis=0)

    def unpack_anchor(s):
        sides = []
        for g in range(2):
            part = s[8 * g:8 * g + 8]
            sides.append(jnp.concatenate([spread_group(part, b) for b in range(ablocks)], axis=0))
        return jnp.concatenate(sides, axis=1)

    dst = iota((ncol, ncol), 1)
    src = iota((ncol, ncol), 0)
    local = dst % half
    side = dst // half
    parity = (core + side) % 2
    wanted = local + (local // piece + parity) * piece
    perm = (src == wanted).astype(F32).astype(BF16)

    def arrange(s):
        large[s].wait()
        block = counts_ref[8 * s:8 * s + 8].reshape(crow, ncol).astype(F32).astype(BF16)
        moved = jnp.dot(block, perm, preferred_element_type=F32)
        outbox[s * crow:(s + 1) * crow] = moved[:, half:]
        vals[core, s * crow:(s + 1) * crow] = moved[:, :half]

    for dma in small:
        dma.wait()
    own_anchor = lax.dot(anchor_ref[...], spread, precision=HIGH)
    weight_row = jnp.sum(jnp.where(
        diag_all, jnp.broadcast_to(to_rows(weight_ref[...], rank), (rank, LANES)), 0.0), axis=0, keepdims=True)
    abuf[core] = own_anchor * weight_row
    ccur[...] = twice(lax.dot_general(hour_ref[...], spread, (((0,), (0,)), ((), ())), precision=HIGH))
    place = (iota((piece, LANES), 1) == zi * piece + iota((piece, LANES), 0)).astype(F32)
    zbuf[0, zi] = jnp.concatenate([
        lax.dot_general(dest_ref[...], place, (((0,), (0,)), ((), ())), precision=HIGH),
        jnp.zeros((8, LANES), F32)], axis=0)

    pl.semaphore_wait(barrier, nx - 1 + nz - 1)

    start(zbuf.at[0], z_send.at[0], z_recv.at[0], zpeers, zi)

    def acopy(slot):
        return pltpu.make_async_remote_copy(
            src_ref=abuf.at[slot], dst_ref=abuf.at[slot], send_sem=a_sem.at[0], recv_sem=a_sem.at[1],
            device_id=partner, device_id_type=MESH)

    acopy(core).start()

    def vcopy(s, slot):
        return pltpu.make_async_remote_copy(
            src_ref=outbox.at[pl.ds(s * crow, crow)],
            dst_ref=vals.at[slot, pl.ds(s * crow, crow)],
            send_sem=v_send.at[s], recv_sem=v_recv.at[s],
            device_id=partner, device_id_type=MESH)

    for s in range(chunks):
        arrange(s)
        vcopy(s, core).start()

    bmod[...] = jnp.zeros_like(bmod)
    balo[...] = jnp.zeros_like(balo)

    def set_right(t):
        hi = t.astype(BF16).astype(F32)
        lo = t - hi
        model = jnp.concatenate([hi] * (copies // 2) + [lo] * (copies // 2), axis=0).astype(BF16)
        along = jnp.concatenate([hi, lo], axis=0).astype(BF16)
        for g in range(2):
            lanes = slice(g * LANES, (g + 1) * LANES)
            bmod[lanes, lanes] = model
            for part in range(2):
                balo[g * 2 * rank:(g + 1) * 2 * rank, (2 * part + g) * LANES:(2 * part + g + 1) * LANES] = along

    high_lane = (iota((1, 2 * LANES), 1) // rank) % 2 == 0

    def ratio_chunk(s):
        left = ucur[8 * s:8 * s + 8]
        rows = slice(s * crow, (s + 1) * crow)
        kh = (left[:, None, :] * ccur[...][None, :, :]).reshape(crow, 2 * LANES)
        hi = kh.astype(BF16).astype(F32)
        khs = jnp.where(high_lane, hi, kh - hi).astype(BF16)
        model = jnp.dot(khs, bmod[...], preferred_element_type=F32)
        values = jnp.concatenate([vals[0, rows], vals[1, rows]], axis=1)
        ratio = values / model
        rh = ratio.astype(BF16)
        rl = (ratio - rh.astype(F32)).astype(BF16)
        return left, khs, rh, rl

    def along_of(rh, rl):
        return lax.dot_general(jnp.concatenate([rh, rl], axis=1), balo[...], (((1,), (1,)), ((), ())),
                               preferred_element_type=F32).reshape(8, nhour, LANES)

    def anchor_phi():
        parts = []
        for s in range(chunks):
            left, khs, rh, rl = ratio_chunk(s)
            parts.append(jnp.sum(along_of(rh, rl) * ccur[:, :LANES][None, :, :], axis=1))
        p = pair_up(jnp.concatenate(parts, axis=0))
        return jnp.concatenate([spread_group(p, 1), spread_group(p, 3)], axis=1)

    def hour_phi():
        p = None
        for s in range(chunks):
            left, khs, rh, rl = ratio_chunk(s)
            mixed = jnp.where(group < 2, left[:, :LANES], left[:, LANES:])
            part = jnp.sum(along_of(rh, rl) * mixed[:, None, :], axis=0)
            p = part if p is None else p + part
        return pair_up(p + pltpu.roll(p, 2 * rank, 1))

    def dest_phi():
        dims = (((0,), (0,)), ((), ()))
        total = None
        for s in range(chunks):
            left, khs, rh, rl = ratio_chunk(s)
            for g in range(2):
                lanes = slice(g * LANES, (g + 1) * LANES)
                for r in (rh, rl):
                    part = lax.dot_general(khs[:, lanes], r[:, lanes], dims, preferred_element_type=F32)
                    total = part if total is None else total + part
        return total[:rank] + total[rank:2 * rank]

    acopy(1 - core).wait_recv()
    ucur[...] = jnp.concatenate([abuf[0], abuf[1]], axis=1)
    gathered = collect(zbuf.at[0], z_recv.at[0], nz)
    tcur[...] = gathered[:rank]
    set_right(tcur[...])
    for s in range(chunks):
        vcopy(s, 1 - core).wait_recv()

    @pl.loop(0, OUTER)
    def _(outer):
        for inner in range(INNER):
            e = outer * 4 + inner
            xb, xs, xr = xbuf.at[e], x_send.at[e], x_recv.at[e]
            xb[xi] = pack_anchor(anchor_phi())
            start(xb, xs, xr, xpeers, xi)
            s = collect(xb, xr, nx)
            ucur[...] = ucur[...] * (unpack_anchor(s) / (nhour * total_cols))
        col = jnp.sum(ucur[...], axis=0, keepdims=True)
        col = col[:, :LANES] + col[:, LANES:]
        anchor_w = None
        for inner in range(INNER):
            e = 1 + outer * 2 + inner
            zb, zs, zr = zbuf.at[e], z_send.at[e], z_recv.at[e]
            zb[zi] = jnp.concatenate([dest_phi(), jnp.broadcast_to(col, (8, LANES))], axis=0)
            start(zb, zs, zr, zpeers, zi)
            s = collect(zb, zr, nz)
            growth = tcur[...] * (s[:rank] / (total_rows * nhour))
            if inner == 0:
                anchor_w = s[rank:rank + 1] / total_rows
                growth = growth / to_column(anchor_w)
            tcur[...] = growth
            set_right(growth)
        ucur[...] = ucur[...] / twice(anchor_w)
        dest_col = to_row(jnp.sum(tcur[...], axis=1, keepdims=True))
        dest_w = None
        for inner in range(INNER):
            e = outer * 4 + 2 + inner
            xb, xs, xr = xbuf.at[e], x_send.at[e], x_recv.at[e]
            xb[xi] = pack_hour(hour_phi(), dest_col)
            start(xb, xs, xr, xpeers, xi)
            s = collect(xb, xr, nx)
            h = outer * 2 + inner
            hb, hs, hr = hbuf.at[h], h_send.at[h], h_recv.at[h]
            hb[zi] = s
            start(hb, hs, hr, zpeers, zi)
            if inner == 0:
                dest_w = spread_group(s[:1], copies - 1) / total_cols
            s = collect(hb, hr, nz)
            growth = ccur[:, :LANES] * (unpack_hour(s) / (total_rows * total_cols))
            if inner == 0:
                growth = growth / dest_w
            ccur[...] = twice(growth)
        w = jnp.sum(ccur[:, :LANES], axis=0, keepdims=True) / nhour
        ccur[...] = ccur[...] / twice(w)
        tcur[...] = tcur[...] / to_column(dest_w)
        weight_out[...] = w[:, :rank]

        @pl.when(outer == OUTER - 1)
        def _():
            mine = jnp.where(core == 0, ucur[:, :LANES], ucur[:, LANES:])
            anchor_out[...] = mine[:, :rank]
            hour_out[...] = lax.dot_general(
                diag.astype(F32), ccur[:, :LANES], (((1,), (1,)), ((), ())), precision=HIGH)
            dest_out[...] = lax.dot_general(
                place, tcur[...], (((1,), (1,)), ((), ())), precision=HIGH)

        @pl.when(outer < OUTER - 1)
        def _():
            ucur[...] = ucur[...] * twice(w)
            set_right(tcur[...])

    acopy(core).wait_send()
    for s in range(chunks):
        vcopy(s, core).wait_send()
    for e in range(OUTER * 4):
        wait_bytes(xbuf.at[e, pl.ds(0, nx - 1)], x_send.at[e])
    for e in range(1 + OUTER * 2):
        wait_bytes(zbuf.at[e, pl.ds(0, nz - 1)], z_send.at[e])
    for e in range(OUTER * 2):
        wait_bytes(hbuf.at[e, pl.ds(0, nz - 1)], h_send.at[e])


def put_out(*refs):
    copies = [pltpu.make_async_copy(refs[q], refs[4 + q], refs[8].at[q]) for q in range(4)]
    for c in copies:
        c.start()
    for c in copies:
        c.wait()


def to_rows(row, rank):
    square = jnp.where(iota((rank, rank), 0) == iota((rank, rank), 1), jnp.broadcast_to(row, (rank, rank)), 0.0)
    return jnp.sum(square, axis=1, keepdims=True)


def on_device(counts, anchor_factor, dest_factor, hour_factor, weights):
    norig = lax.axis_size("orig")
    ndest = lax.axis_size("dest")
    nz, nx = norig // 2, 2 * ndest
    nrow, nhour, ncol = counts.shape
    rank = hour_factor.shape[1]
    rows = nrow * nhour
    chunks = nrow // 8
    hrow = -(-nhour // (8 * (LANES // rank - 1))) * 8
    dma = pltpu.SemaphoreType.DMA
    vmem = pltpu.VMEM
    outs = pl.pallas_call(
        functools.partial(kernel, nz, ndest),
        out_shape=[
            jax.ShapeDtypeStruct(anchor_factor.shape, F32),
            jax.ShapeDtypeStruct(dest_factor.shape, F32),
            jax.ShapeDtypeStruct((rank, nhour), F32),
            jax.ShapeDtypeStruct((1, rank), F32),
        ],
        in_specs=[pl.BlockSpec(memory_space=pltpu.HBM)] * 5,
        out_specs=[pl.BlockSpec(memory_space=pltpu.VMEM)] * 4,
        scratch_shapes=[
            vmem((2, rows, LANES), F32),
            vmem((rows, LANES), F32),
            vmem((nrow, 2 * LANES), F32),
            vmem((nhour, 2 * LANES), F32),
            vmem((rank, LANES), F32),
            vmem((2 * LANES, 2 * LANES), BF16),
            vmem((4 * rank, 4 * LANES), BF16),
            vmem((OUTER * 4, nx, hrow, LANES), F32),
            vmem((1 + OUTER * 2, nz, rank + 8, LANES), F32),
            vmem((OUTER * 2, nz, hrow, LANES), F32),
            vmem((2, nrow, LANES), F32),
            vmem(counts.shape, counts.dtype),
            vmem(anchor_factor.shape, F32),
            vmem(dest_factor.shape, F32),
            vmem((rank, nhour), F32),
            vmem((1, rank), F32),
            dma((OUTER * 4,)), dma((OUTER * 4,)),
            dma((1 + OUTER * 2,)), dma((1 + OUTER * 2,)),
            dma((OUTER * 2,)), dma((OUTER * 2,)),
            dma((chunks,)), dma((chunks,)), dma((2,)), dma((4 + chunks,)),
        ],
        compiler_params=pltpu.CompilerParams(
            collective_id=0, has_side_effects=True, vmem_limit_bytes=67043328),
    )(counts, anchor_factor, dest_factor, hour_factor.T, weights.reshape(1, rank))
    outs = pl.pallas_call(
        put_out,
        out_shape=[jax.ShapeDtypeStruct(o.shape, F32) for o in outs],
        in_specs=[pl.BlockSpec(memory_space=pltpu.VMEM)] * 4,
        out_specs=[pl.BlockSpec(memory_space=pltpu.HBM)] * 4,
        scratch_shapes=[dma((4,))],
    )(*outs)
    return outs[0], outs[1], outs[2].T, outs[3].reshape(rank)


def solution(mesh):
    return jax.shard_map(
        on_device,
        mesh=mesh,
        in_specs=(P("orig", None, "dest"), P("orig", None), P(("dest", "orig"), None), P(), P()),
        out_specs=(P("orig", None), P(("dest", "orig"), None), P(), P()),
        check_vma=False,
    )
```

```python
import functools

import jax
import jax.numpy as jnp
from jax import lax
from jax.experimental import pallas as pl
from jax.experimental.pallas import tpu as pltpu
from jax.sharding import PartitionSpec as P

INNER = 2
OUTER = 2
LANES = 128
F32 = jnp.float32
BF16 = jnp.bfloat16
HIGH = lax.Precision.HIGHEST
MESH = pl.DeviceIdType.MESH


def iota(shape, dim):
    return lax.broadcasted_iota(jnp.int32, shape, dim)


def kernel(nz, ndest, counts_in, anchor_in, dest_in, hour_in, weight_in,
           anchor_out, dest_out, hour_out, weight_out,
           vals, outbox, ucur, ccur, tcur, bmod, balo,
           ubuf, xbuf, zbuf, hbuf, abuf, counts_ref, anchor_ref, dest_ref, hour_ref, weight_ref,
           u_send, u_recv, x_send, x_recv, z_send, z_recv, h_send, h_recv, v_send, v_recv, a_sem, in_sem):
    nrow, nhour, ncol = counts_ref.shape
    rank = hour_ref.shape[0]
    piece = dest_ref.shape[0]
    copies = LANES // rank
    half = ncol // 2
    nx = 2 * ndest
    total_rows = nrow * 2 * nz
    total_cols = ncol * ndest
    me_orig = lax.axis_index("orig")
    me_dest = lax.axis_index("dest")
    zi = me_orig // 2
    core = me_orig % 2
    xi = me_dest * 2 + core
    partner = {"orig": zi * 2 + (1 - core)}
    chunks = vals.shape[1] // (8 * nhour)
    crow = 8 * nhour

    xpeers = []
    for t in range(1, nx):
        idx = (xi + t) % nx
        xpeers.append({"orig": zi * 2 + idx % 2, "dest": idx // 2})
    zpeers = [{"orig": (zi + t) % nz * 2 + core} for t in range(1, nz)]

    small = [pltpu.make_async_copy(a, b, in_sem.at[q]) for q, (a, b) in enumerate(
        ((anchor_in, anchor_ref), (dest_in, dest_ref), (hour_in, hour_ref), (weight_in, weight_ref)))]
    large = [pltpu.make_async_copy(counts_in.at[pl.ds(8 * s, 8)], counts_ref.at[pl.ds(8 * s, 8)], in_sem.at[4 + s])
             for s in range(chunks)]
    for dma in small + large:
        dma.start()
    barrier = pltpu.get_barrier_semaphore()
    for who in zpeers + xpeers:
        pl.semaphore_signal(barrier, inc=1, device_id=who, device_id_type=MESH)

    def start(ref, send, recv, peers, me):
        for who in peers:
            pltpu.make_async_remote_copy(
                src_ref=ref.at[me], dst_ref=ref.at[me], send_sem=send, recv_sem=recv,
                device_id=who, device_id_type=MESH).start()

    def wait_bytes(ref, sem):
        pltpu.make_async_copy(ref, ref, sem).wait()

    def collect(ref, recv, n):
        wait_bytes(ref.at[pl.ds(0, n - 1)], recv)
        total = ref[0]
        for s in range(1, n):
            total = total + ref[s]
        return total

    lane = iota((1, LANES), 1)
    group = lane // rank
    spread = (iota((rank, LANES), 1) % rank == iota((rank, LANES), 0)).astype(F32)
    diag = iota((rank, LANES), 1) == iota((rank, LANES), 0)
    diag_all = iota((rank, LANES), 1) % rank == iota((rank, LANES), 0)

    def to_column(row):
        return jnp.sum(jnp.where(diag, jnp.broadcast_to(row, (rank, LANES)), 0.0), axis=1, keepdims=True)

    def to_row(column):
        return jnp.sum(jnp.where(diag_all, jnp.broadcast_to(column, (rank, LANES)), 0.0), axis=0, keepdims=True)

    def spread_group(x, b):
        x = jnp.where(group == b, x, 0.0)
        step = rank
        while step < LANES:
            x = x + pltpu.roll(x, step, 1)
            step *= 2
        return x

    def pair_up(x):
        return x + pltpu.roll(x, rank, 1)

    def twice(x):
        return jnp.concatenate([x, x], axis=1)

    hrow = -(-nhour // (8 * (copies - 1))) * 8
    hblocks = nhour // hrow

    def pack_hour(p, extra):
        out = jnp.broadcast_to(extra, (hrow, LANES))
        for b in range(hblocks):
            out = jnp.where(group == b, p[b * hrow:(b + 1) * hrow], out)
        return out

    def unpack_hour(s):
        return jnp.concatenate([spread_group(s, b) for b in range(hblocks)], axis=0)

    dst = iota((ncol, ncol), 1)
    src = iota((ncol, ncol), 0)
    local = dst % half
    side = dst // half
    parity = (core + side) % 2
    wanted = local + (local // piece + parity) * piece
    perm = (src == wanted).astype(F32).astype(BF16)

    def arrange(s):
        large[s].wait()
        block = counts_ref[8 * s:8 * s + 8].reshape(crow, ncol).astype(F32).astype(BF16)
        moved = jnp.dot(block, perm, preferred_element_type=F32)
        outbox[s * crow:(s + 1) * crow] = moved[:, half:]
        vals[core, s * crow:(s + 1) * crow] = moved[:, :half]

    for dma in small:
        dma.wait()
    own_anchor = lax.dot(anchor_ref[...], spread, precision=HIGH)
    weight_row = jnp.sum(jnp.where(
        diag_all, jnp.broadcast_to(to_rows(weight_ref[...], rank), (rank, LANES)), 0.0), axis=0, keepdims=True)
    abuf[core] = own_anchor * weight_row
    ccur[...] = twice(lax.dot_general(hour_ref[...], spread, (((0,), (0,)), ((), ())), precision=HIGH))
    place = (iota((piece, LANES), 1) == zi * piece + iota((piece, LANES), 0)).astype(F32)
    zbuf[0, zi] = jnp.concatenate([
        lax.dot_general(dest_ref[...], place, (((0,), (0,)), ((), ())), precision=HIGH),
        jnp.zeros((8, LANES), F32)], axis=0)

    pl.semaphore_wait(barrier, nx - 1 + nz - 1)

    start(zbuf.at[0], z_send.at[0], z_recv.at[0], zpeers, zi)

    def acopy(slot):
        return pltpu.make_async_remote_copy(
            src_ref=abuf.at[slot], dst_ref=abuf.at[slot], send_sem=a_sem.at[0], recv_sem=a_sem.at[1],
            device_id=partner, device_id_type=MESH)

    acopy(core).start()

    def vcopy(s, slot):
        return pltpu.make_async_remote_copy(
            src_ref=outbox.at[pl.ds(s * crow, crow)],
            dst_ref=vals.at[slot, pl.ds(s * crow, crow)],
            send_sem=v_send.at[s], recv_sem=v_recv.at[s],
            device_id=partner, device_id_type=MESH)

    for s in range(chunks):
        arrange(s)
        vcopy(s, core).start()

    bmod[...] = jnp.zeros_like(bmod)
    balo[...] = jnp.zeros_like(balo)

    def set_right(t):
        hi = t.astype(BF16).astype(F32)
        lo = t - hi
        model = jnp.concatenate([hi] * (copies // 2) + [lo] * (copies // 2), axis=0).astype(BF16)
        along = jnp.concatenate([hi, lo], axis=0).astype(BF16)
        for g in range(2):
            lanes = slice(g * LANES, (g + 1) * LANES)
            bmod[lanes, lanes] = model
            for part in range(2):
                balo[g * 2 * rank:(g + 1) * 2 * rank, (2 * part + g) * LANES:(2 * part + g + 1) * LANES] = along

    high_lane = (iota((1, 2 * LANES), 1) // rank) % 2 == 0

    def ratio_chunk(s):
        left = ucur[8 * s:8 * s + 8]
        rows = slice(s * crow, (s + 1) * crow)
        kh = (left[:, None, :] * ccur[...][None, :, :]).reshape(crow, 2 * LANES)
        hi = kh.astype(BF16).astype(F32)
        khs = jnp.where(high_lane, hi, kh - hi).astype(BF16)
        model = jnp.dot(khs, bmod[...], preferred_element_type=F32)
        values = jnp.concatenate([vals[0, rows], vals[1, rows]], axis=1)
        ratio = values / model
        rh = ratio.astype(BF16)
        rl = (ratio - rh.astype(F32)).astype(BF16)
        return left, khs, rh, rl

    def along_of(rh, rl):
        return lax.dot_general(jnp.concatenate([rh, rl], axis=1), balo[...], (((1,), (1,)), ((), ())),
                               preferred_element_type=F32).reshape(8, nhour, LANES)

    def anchor_step(e, before):
        for s in range(chunks):
            before(s)
            left, khs, rh, rl = ratio_chunk(s)
            p = pair_up(jnp.sum(along_of(rh, rl) * ccur[:, :LANES][None, :, :], axis=1))
            ub = ubuf.at[e * chunks + s]
            ub[xi] = p
            start(ub, u_send.at[e * chunks + s], u_recv.at[e * chunks + s], xpeers, xi)

    def anchor_update(e):
        def update(s):
            p = collect(ubuf.at[e * chunks + s], u_recv.at[e * chunks + s], nx)
            p = jnp.concatenate([spread_group(p, 1), spread_group(p, 3)], axis=1)
            rows = slice(8 * s, 8 * s + 8)
            ucur[rows] = ucur[rows] * (p / (nhour * total_cols))
        return update

    def hour_phi():
        p = None
        for s in range(chunks):
            left, khs, rh, rl = ratio_chunk(s)
            mixed = jnp.where(group < 2, left[:, :LANES], left[:, LANES:])
            part = jnp.sum(along_of(rh, rl) * mixed[:, None, :], axis=0)
            p = part if p is None else p + part
        return pair_up(p + pltpu.roll(p, 2 * rank, 1))

    def dest_phi(before):
        dims = (((0,), (0,)), ((), ()))
        total = None
        for s in range(chunks):
            before(s)
            left, khs, rh, rl = ratio_chunk(s)
            for g in range(2):
                lanes = slice(g * LANES, (g + 1) * LANES)
                for r in (rh, rl):
                    part = lax.dot_general(khs[:, lanes], r[:, lanes], dims, preferred_element_type=F32)
                    total = part if total is None else total + part
        return total[:rank] + total[rank:2 * rank]

    acopy(1 - core).wait_recv()
    ucur[...] = jnp.concatenate([abuf[0], abuf[1]], axis=1)
    gathered = collect(zbuf.at[0], z_recv.at[0], nz)
    tcur[...] = gathered[:rank]
    set_right(tcur[...])
    for s in range(chunks):
        vcopy(s, 1 - core).wait_recv()

    @pl.loop(0, OUTER)
    def _(outer):
        before = lambda s: None
        for inner in range(INNER):
            anchor_step(outer * INNER + inner, before)
            before = anchor_update(outer * INNER + inner)
        anchor_w = None
        for inner in range(INNER):
            e = 1 + outer * 2 + inner
            zb, zs, zr = zbuf.at[e], z_send.at[e], z_recv.at[e]
            p = dest_phi(before)
            before = lambda s: None
            col = jnp.sum(ucur[...], axis=0, keepdims=True)
            col = col[:, :LANES] + col[:, LANES:]
            zb[zi] = jnp.concatenate([p, jnp.broadcast_to(col, (8, LANES))], axis=0)
            start(zb, zs, zr, zpeers, zi)
            s = collect(zb, zr, nz)
            growth = tcur[...] * (s[:rank] / (total_rows * nhour))
            if inner == 0:
                anchor_w = s[rank:rank + 1] / total_rows
                growth = growth / to_column(anchor_w)
            tcur[...] = growth
            set_right(growth)
        ucur[...] = ucur[...] / twice(anchor_w)
        dest_col = to_row(jnp.sum(tcur[...], axis=1, keepdims=True))
        dest_w = None
        for inner in range(INNER):
            e = outer * 2 + inner
            xb, xs, xr = xbuf.at[e], x_send.at[e], x_recv.at[e]
            xb[xi] = pack_hour(hour_phi(), dest_col)
            start(xb, xs, xr, xpeers, xi)
            s = collect(xb, xr, nx)
            h = outer * 2 + inner
            hb, hs, hr = hbuf.at[h], h_send.at[h], h_recv.at[h]
            hb[zi] = s
            start(hb, hs, hr, zpeers, zi)
            if inner == 0:
                dest_w = spread_group(s[:1], copies - 1) / total_cols
            s = collect(hb, hr, nz)
            growth = ccur[:, :LANES] * (unpack_hour(s) / (total_rows * total_cols))
            if inner == 0:
                growth = growth / dest_w
            ccur[...] = twice(growth)
        w = jnp.sum(ccur[:, :LANES], axis=0, keepdims=True) / nhour
        ccur[...] = ccur[...] / twice(w)
        tcur[...] = tcur[...] / to_column(dest_w)
        weight_out[...] = w[:, :rank]

        @pl.when(outer == OUTER - 1)
        def _():
            mine = jnp.where(core == 0, ucur[:, :LANES], ucur[:, LANES:])
            anchor_out[...] = mine[:, :rank]
            hour_out[...] = lax.dot_general(
                diag.astype(F32), ccur[:, :LANES], (((1,), (1,)), ((), ())), precision=HIGH)
            dest_out[...] = lax.dot_general(
                place, tcur[...], (((1,), (1,)), ((), ())), precision=HIGH)

        @pl.when(outer < OUTER - 1)
        def _():
            ucur[...] = ucur[...] * twice(w)
            set_right(tcur[...])

    acopy(core).wait_send()
    for s in range(chunks):
        vcopy(s, core).wait_send()
    for e in range(OUTER * INNER * chunks):
        wait_bytes(ubuf.at[e, pl.ds(0, nx - 1)], u_send.at[e])
    for e in range(OUTER * 2):
        wait_bytes(xbuf.at[e, pl.ds(0, nx - 1)], x_send.at[e])
    for e in range(1 + OUTER * 2):
        wait_bytes(zbuf.at[e, pl.ds(0, nz - 1)], z_send.at[e])
    for e in range(OUTER * 2):
        wait_bytes(hbuf.at[e, pl.ds(0, nz - 1)], h_send.at[e])


def put_out(*refs):
    copies = [pltpu.make_async_copy(refs[q], refs[4 + q], refs[8].at[q]) for q in range(4)]
    for c in copies:
        c.start()
    for c in copies:
        c.wait()


def to_rows(row, rank):
    square = jnp.where(iota((rank, rank), 0) == iota((rank, rank), 1), jnp.broadcast_to(row, (rank, rank)), 0.0)
    return jnp.sum(square, axis=1, keepdims=True)


def on_device(counts, anchor_factor, dest_factor, hour_factor, weights):
    norig = lax.axis_size("orig")
    ndest = lax.axis_size("dest")
    nz, nx = norig // 2, 2 * ndest
    nrow, nhour, ncol = counts.shape
    rank = hour_factor.shape[1]
    rows = nrow * nhour
    chunks = nrow // 8
    hrow = -(-nhour // (8 * (LANES // rank - 1))) * 8
    dma = pltpu.SemaphoreType.DMA
    vmem = pltpu.VMEM
    outs = pl.pallas_call(
        functools.partial(kernel, nz, ndest),
        out_shape=[
            jax.ShapeDtypeStruct(anchor_factor.shape, F32),
            jax.ShapeDtypeStruct(dest_factor.shape, F32),
            jax.ShapeDtypeStruct((rank, nhour), F32),
            jax.ShapeDtypeStruct((1, rank), F32),
        ],
        in_specs=[pl.BlockSpec(memory_space=pltpu.HBM)] * 5,
        out_specs=[pl.BlockSpec(memory_space=pltpu.VMEM)] * 4,
        scratch_shapes=[
            vmem((2, rows, LANES), F32),
            vmem((rows, LANES), F32),
            vmem((nrow, 2 * LANES), F32),
            vmem((nhour, 2 * LANES), F32),
            vmem((rank, LANES), F32),
            vmem((2 * LANES, 2 * LANES), BF16),
            vmem((4 * rank, 4 * LANES), BF16),
            vmem((OUTER * INNER * chunks, nx, 8, LANES), F32),
            vmem((OUTER * 2, nx, hrow, LANES), F32),
            vmem((1 + OUTER * 2, nz, rank + 8, LANES), F32),
            vmem((OUTER * 2, nz, hrow, LANES), F32),
            vmem((2, nrow, LANES), F32),
            vmem(counts.shape, counts.dtype),
            vmem(anchor_factor.shape, F32),
            vmem(dest_factor.shape, F32),
            vmem((rank, nhour), F32),
            vmem((1, rank), F32),
            dma((OUTER * INNER * chunks,)), dma((OUTER * INNER * chunks,)),
            dma((OUTER * 2,)), dma((OUTER * 2,)),
            dma((1 + OUTER * 2,)), dma((1 + OUTER * 2,)),
            dma((OUTER * 2,)), dma((OUTER * 2,)),
            dma((chunks,)), dma((chunks,)), dma((2,)), dma((4 + chunks,)),
        ],
        compiler_params=pltpu.CompilerParams(
            collective_id=0, has_side_effects=True, vmem_limit_bytes=67043328),
    )(counts, anchor_factor, dest_factor, hour_factor.T, weights.reshape(1, rank))
    outs = pl.pallas_call(
        put_out,
        out_shape=[jax.ShapeDtypeStruct(o.shape, F32) for o in outs],
        in_specs=[pl.BlockSpec(memory_space=pltpu.VMEM)] * 4,
        out_specs=[pl.BlockSpec(memory_space=pltpu.HBM)] * 4,
        scratch_shapes=[dma((4,))],
    )(*outs)
    return outs[0], outs[1], outs[2].T, outs[3].reshape(rank)


def solution(mesh):
    return jax.shard_map(
        on_device,
        mesh=mesh,
        in_specs=(P("orig", None, "dest"), P("orig", None), P(("dest", "orig"), None), P(), P()),
        out_specs=(P("orig", None), P(("dest", "orig"), None), P(), P()),
        check_vma=False,
    )
```
